32 devices in a mesh: grp: 2 (over y), node: 4 (over z), head: 4 (over x, core).
Axes of the slice: x: 2, y: 2, z: 4, core: 2. Of those that a mesh axis runs over, the one named last changes fastest.
Arguments:
- queries: bfloat16 [2048, 1024], P(('grp', 'node', 'head')), parts along dimension 0, may hold values from -8 to 8
- key_rows: bfloat16 [2048, 1024], P(('grp', 'node', 'head')), parts along dimension 0, may hold values from -8 to 8
- value_rows: bfloat16 [2048, 1024], P(('grp', 'node', 'head')), parts along dimension 0, may hold values from -6 to 6
- out_grads: bfloat16 [2048, 1024], P(('grp', 'node', 'head')), parts along dimension 0, may hold values from -6 to 6
- neighbours: int32 [16, 8], P('grp'), parts along dimension 0, may hold values from 0 to 7, as said below
Outputs:
- attended: bfloat16 [2048, 1024], P(('grp', 'node', 'head')), parts along dimension 0
- query_grad: bfloat16 [2048, 1024], P(('grp', 'node', 'head')), parts along dimension 0
- key_grad: bfloat16 [2048, 1024], P(('grp', 'node', 'head')), parts along dimension 0
- value_grad: bfloat16 [2048, 1024], P(('grp', 'node', 'head')), parts along dimension 0
The draws below stay inside these ranges and needn't reach their ends.
There are 2 independent parts, one for each index of `grp`. The reference program is written for one: setup_inputs(seed, part) draws one part's arguments, and reference() takes and returns one part's arrays. A program takes and returns all parts, laid end to end along the dimension named above; each array names one. Nothing has to cross between parts.
Inputs may be any that keep to these rules, and one draw needn't show every extreme that they name: `neighbours`: the owner of patch p is p // 2. Every listed neighbour of a patch has an owner at distance at most 1 from the patch's owner. The patches of one owner together list exactly 1 distinct patches of each other owner within distance 1 that exists, and none of any other owner.
All inputs are finite; a program needn't handle non-finite values.
Results may differ from the reference program's by a relative error of at most 0.012.
Values may be sent and summed in bfloat16 or wider, within the bound.
A program may use at most 64 MiB of HBM per device.

```python
import math
import jax
import jax.numpy as jnp
from jax import lax

HEADS = 16
HEAD_DIM = 64
PATCH = 128
NBRS = 8
RADIUS = 1
CAP = 1
PATCH_DEV = 2
D = 1024
PATCHES = 8
NODES = 1024


def draw_queries(key, part):
    inner = jax.random.fold_in(key, 1)
    field = jnp.clip(jax.random.normal(inner, (PATCHES, PATCH, HEADS, HEAD_DIM)), -6.0, 6.0)
    return field.reshape(NODES, D).astype(jnp.bfloat16)


def draw_key_rows(key, part):
    inner = jax.random.fold_in(key, 2)
    field = jnp.clip(jax.random.normal(inner, (PATCHES, PATCH, HEADS, HEAD_DIM)), -6.0, 6.0)
    return field.reshape(NODES, D).astype(jnp.bfloat16)


def draw_neighbours(key, part):
    owners = PATCHES // PATCH_DEV
    inner = jax.random.fold_in(key, 3)
    key_rank, key_turn, key_near = jax.random.split(inner, 3)
    directions = 2 * RADIUS
    offsets = jnp.array(list(range(-RADIUS, 0)) + list(range(1, RADIUS + 1)), jnp.int32)
    rank_keys = jax.random.randint(key_rank, (owners, directions, PATCH_DEV), 0, 1 << 20) * PATCH_DEV + jnp.arange(PATCH_DEV, dtype=jnp.int32)
    ordering = jnp.argsort(rank_keys, axis=-1).astype(jnp.int32)
    rotate = jax.random.randint(key_turn, (owners, directions, 1), 0, CAP)
    picked = (jnp.arange(PATCH_DEV, dtype=jnp.int32)[None, None, :] + rotate) % CAP
    chosen = jnp.take_along_axis(ordering, picked, axis=-1)
    target = jnp.arange(owners, dtype=jnp.int32)[:, None] + offsets[None, :]
    inside_mesh = (target >= 0) & (target < owners)
    remote = jnp.transpose(target[:, :, None] * PATCH_DEV + chosen, (0, 2, 1))
    inside_mesh = jnp.broadcast_to(inside_mesh[:, None, :], remote.shape)
    nearby = jax.random.randint(key_near, (owners, PATCH_DEV, NBRS), 0, PATCH_DEV) + jnp.arange(owners, dtype=jnp.int32)[:, None, None] * PATCH_DEV
    leading = jnp.where(inside_mesh, remote, nearby[:, :, :directions])
    return jnp.concatenate([leading, nearby[:, :, directions:]], -1).reshape(PATCHES, NBRS).astype(jnp.int32)


def shard_levels(stream_key, shape, pieces, smallest, largest):
    level = 1.0
    for axis_at, blocks in pieces:
        steps = jax.random.uniform(jax.random.fold_in(jax.random.fold_in(stream_key, 6), axis_at), (blocks,), jnp.float32, smallest / len(pieces), largest / len(pieces))
        level = level * jnp.repeat(jnp.exp(steps), shape[axis_at] // blocks).reshape((-1,) + (1,) * (len(shape) - 1 - axis_at))
    return level


def bell_draw(stream_key, shape, deviation, bound, shards=(), kind=jnp.bfloat16):
    values = deviation * jax.random.normal(stream_key, shape, jnp.float32)
    if shards:
        values = values * shard_levels(stream_key, shape, shards, -0.22, 0.18)
    return jnp.clip(values, -bound, bound).astype(kind)


def setup_inputs(seed: int = 0, part: int = 0) -> dict:
    keys = jax.random.split(jax.random.key(seed), 6)
    part_splits = jax.random.split(jax.random.fold_in(keys[5], part), 6)
    return {
        "queries": draw_queries(jax.random.fold_in(jax.random.fold_in(keys[5], part), 71), part),
        "key_rows": draw_key_rows(jax.random.fold_in(jax.random.fold_in(keys[5], part), 71), part),
        "value_rows": bell_draw(part_splits[2], (NODES, D), 1.0, 6.0, ((0, 16),)),
        "out_grads": bell_draw(part_splits[3], (NODES, D), 1.0, 6.0, ((0, 16),)),
        "neighbours": draw_neighbours(jax.random.fold_in(jax.random.fold_in(keys[5], part), 71), part),
    }


def to_low(values_in):
    return lax.optimization_barrier(values_in.astype(jnp.bfloat16)).astype(jnp.float32)


def attend_block(query_blk, grad_blk, key_blk, value_blk):
    score_scale = HEAD_DIM ** -0.5
    query_f = query_blk.astype(jnp.float32)
    grad_f = grad_blk.astype(jnp.float32)
    key_f = key_blk.astype(jnp.float32)
    value_f = value_blk.astype(jnp.float32)
    scores = jnp.einsum("bqhd,bkhd->bhqk", query_f, key_f) * score_scale
    row_max = jnp.max(scores, -1, keepdims=True)
    exp_scores = jnp.exp(scores - row_max)
    weights = exp_scores / jnp.sum(exp_scores, -1, keepdims=True)
    weights_low = to_low(weights)
    mixed = jnp.einsum("bhqk,bkhd->bqhd", weights_low, value_f)
    grad_weights = jnp.einsum("bqhd,bkhd->bhqk", grad_f, value_f)
    row_dots = jnp.transpose(jnp.sum(grad_f * mixed, -1), (0, 2, 1))[..., None]
    grad_scores = to_low(weights * (grad_weights - row_dots))
    query_grad = (jnp.einsum("bhqk,bkhd->bqhd", grad_scores, key_f) * score_scale).astype(jnp.bfloat16)
    key_grad = jnp.einsum("bhqk,bqhd->bkhd", grad_scores, query_f) * score_scale
    value_grad = jnp.einsum("bhqk,bqhd->bkhd", weights_low, grad_f)
    return mixed.astype(jnp.bfloat16), query_grad, key_grad, value_grad


def reference(queries, key_rows, value_rows, out_grads, neighbours):
    patches = neighbours.shape[0]
    shape_four = (patches, PATCH, HEADS, HEAD_DIM)
    query_four = queries.reshape(shape_four)
    key_four = key_rows.reshape(shape_four)
    value_four = value_rows.reshape(shape_four)
    grad_four = out_grads.reshape(shape_four)
    key_index = jnp.concatenate([jnp.arange(patches, dtype=jnp.int32)[:, None], neighbours.astype(jnp.int32)], 1)
    block = math.gcd(patches, max(1, 512 // PATCH))
    block_count = patches // block
    span = (NBRS + 1) * PATCH

    def one_block(carry, inputs):
        key_acc, value_acc = carry
        query_blk, grad_blk, index_blk = inputs
        flat_index = index_blk.reshape(-1)
        key_blk = jnp.take(key_four, flat_index, axis=0).reshape(block, span, HEADS, HEAD_DIM)
        value_blk = jnp.take(value_four, flat_index, axis=0).reshape(block, span, HEADS, HEAD_DIM)
        mixed, query_grad, key_grad, value_grad = attend_block(query_blk, grad_blk, key_blk, value_blk)
        key_acc = key_acc.at[flat_index].add(key_grad.reshape(block * (NBRS + 1), PATCH, HEADS, HEAD_DIM))
        value_acc = value_acc.at[flat_index].add(value_grad.reshape(block * (NBRS + 1), PATCH, HEADS, HEAD_DIM))
        return (key_acc, value_acc), (mixed, query_grad)

    zeros_acc = jnp.zeros(shape_four, jnp.float32)
    inputs = (query_four.reshape(block_count, block, PATCH, HEADS, HEAD_DIM),
              grad_four.reshape(block_count, block, PATCH, HEADS, HEAD_DIM),
              key_index.reshape(block_count, block, NBRS + 1))
    (key_acc, value_acc), (mixed_all, qgrad_all) = lax.scan(one_block, (zeros_acc, zeros_acc), inputs)
    total = patches * PATCH
    width = HEADS * HEAD_DIM
    return (mixed_all.reshape(total, width), qgrad_all.reshape(total, width),
            key_acc.reshape(total, width).astype(jnp.bfloat16), value_acc.reshape(total, width).astype(jnp.bfloat16))
```

```python
import functools
import math

import jax
import jax.numpy as jnp
from jax import lax
from jax.experimental import pallas as pl
from jax.experimental.pallas import tpu as pltpu
from jax.sharding import PartitionSpec as P

HEAD_DIM = 64
PATCH = 128
LANES = 128
MESH = pl.DeviceIdType.MESH
SCALE = HEAD_DIM ** (-0.5)
LOG2E = math.log2(math.e)
BF16 = jnp.bfloat16
F32 = jnp.float32


def dot(a, b):
    return jnp.dot(a, b, preferred_element_type=F32)


def kernel(
    heads, nodes, nbr_hbm, q_hbm, k_hbm, v_hbm, g_hbm,
    att_hbm, dq_hbm, dk_hbm, dv_hbm,
    nbr_ref, nbr_sem, pool, rows_in, halo_out, grad_out, grad_in, local_grad, result, turned, near,
    in_send, in_recv, halo_send, halo_recv, grad_send, grad_recv, out_send, out_recv,
):
    me = lax.axis_index("head")
    node = lax.axis_index("node")
    has_left, has_right = node > 0, node < nodes - 1
    chunks = pool.shape[1]
    part = q_hbm.shape[0]
    own = part * heads
    patches = own // PATCH
    listed = nbr_ref.shape[1]
    width = chunks * LANES
    peers = [lax.rem(me + d, heads) for d in range(1, heads)]
    sides = ((0, node - 1, has_left), (1, node + 1, has_right))

    lists = pltpu.make_async_copy(nbr_hbm, nbr_ref, nbr_sem)
    lists.start()
    barrier = pltpu.get_barrier_semaphore()
    for peer in peers:
        pl.semaphore_signal(barrier, inc=1, device_id={"head": peer}, device_id_type=MESH)
    for _, other, there in sides:
        @pl.when(there)
        def _():
            pl.semaphore_signal(barrier, inc=1, device_id={"node": other}, device_id_type=MESH)

    sources = (k_hbm, v_hbm, q_hbm, g_hbm)

    def landing(t, c):
        if t < 2:
            return pool.at[t, c, pl.ds(pl.multiple_of(PATCH + me * part, part), part), :]
        return rows_in.at[t - 2, c, pl.ds(pl.multiple_of(me * part, part), part), :]

    def in_copy(t, c, d):
        peer = peers[d]
        cols = pl.ds(pl.multiple_of(peer * width + c * LANES, LANES), LANES)
        return pltpu.make_async_remote_copy(
            src_ref=sources[t].at[:, cols], dst_ref=landing(t, c),
            send_sem=in_send, recv_sem=in_recv.at[t, c],
            device_id={"head": peer}, device_id_type=MESH,
        )

    def in_own(t, c):
        cols = pl.ds(pl.multiple_of(me * width + c * LANES, LANES), LANES)
        return pltpu.make_async_copy(sources[t].at[:, cols], landing(t, c), in_recv.at[t, c])

    order = [(t, c) for ts in ((0, 1), (2, 3)) for c in range(chunks) for t in ts]
    for t, c in order:
        in_own(t, c).start()

    for side, _, there in sides:
        @pl.when(jnp.logical_not(there))
        def _():
            start = side * (PATCH + own)
            pool[:, :, start:start + PATCH, :] = jnp.zeros((2, chunks, PATCH, LANES), BF16)
            grad_in[:, :, side] = jnp.zeros((2, chunks, PATCH, LANES), BF16)

    pl.semaphore_wait(
        barrier, heads - 1 + has_left.astype(jnp.int32) + has_right.astype(jnp.int32)
    )
    for t, c in order:
        for d in range(heads - 1):
            in_copy(t, c, d).start()

    lists.wait()
    first = node * patches
    lane = lax.broadcasted_iota(jnp.int32, (1, own), 1)
    slot_counts = [jnp.zeros((1, own), F32) for _ in range(patches + 2)]
    for p in range(patches):
        counts = [jnp.int32(0)] * (patches + 2)
        counts[1 + p] = jnp.int32(1)
        for e in range(listed):
            value = nbr_ref[first + p, e]
            counts[0] += jnp.where(value < first, 1, 0)
            counts[-1] += jnp.where(value >= first + patches, 1, 0)
            for o in range(patches):
                counts[1 + o] += jnp.where(value == first + o, 1, 0)
        in_patch = (lane >= p * PATCH) & (lane < (p + 1) * PATCH)
        for s in range(patches + 2):
            slot_counts[s] = jnp.where(in_patch, counts[s].astype(F32), slot_counts[s])
    wanted = []
    for side, other, there in sides:
        start = jnp.clip(other, 0, nodes - 1) * patches
        pick = jnp.int32(0)
        for p in range(patches):
            for e in range(listed):
                value = nbr_ref[start + p, e]
                for o in range(1, patches):
                    pick = jnp.maximum(pick, jnp.where(value == first + o, o, 0))
        wanted.append(pick)

    def in_wait(t, c):
        if t < 2:
            whole = pool.at[t, c, pl.ds(PATCH, own), :]
        else:
            whole = rows_in.at[t - 2, c]
        pltpu.make_async_copy(whole, whole, in_recv.at[t, c]).wait()

    def halo_copy(t, c, side, other):
        start = (1 - side) * (PATCH + own)
        return pltpu.make_async_remote_copy(
            src_ref=halo_out.at[side, t, c], dst_ref=pool.at[t, c, pl.ds(start, PATCH), :],
            send_sem=halo_send.at[side], recv_sem=halo_recv.at[t, c, 1 - side],
            device_id={"node": other}, device_id_type=MESH,
        )

    def halo_arrived(t, c, side, other):
        start = side * (PATCH + own)
        return pltpu.make_async_remote_copy(
            src_ref=halo_out.at[side, t, c], dst_ref=pool.at[t, c, pl.ds(start, PATCH), :],
            send_sem=halo_send.at[side], recv_sem=halo_recv.at[t, c, side],
            device_id={"node": other}, device_id_type=MESH,
        )

    def grad_copy(t, c, side, other, arrived=False):
        far = side if arrived else 1 - side
        return pltpu.make_async_remote_copy(
            src_ref=grad_out.at[side, t, c], dst_ref=grad_in.at[t, c, far],
            send_sem=grad_send.at[side], recv_sem=grad_recv.at[t, c, far],
            device_id={"node": other}, device_id_type=MESH,
        )

    outs = (att_hbm, dq_hbm, dk_hbm, dv_hbm)

    def out_copy(t, c, d):
        peer = peers[d]
        cols = pl.ds(pl.multiple_of(me * width + c * LANES, LANES), LANES)
        return pltpu.make_async_remote_copy(
            src_ref=result.at[t, c, pl.ds(pl.multiple_of(peer * part, part), part), :],
            dst_ref=outs[t].at[:, cols],
            send_sem=out_send, recv_sem=out_recv,
            device_id={"head": peer}, device_id_type=MESH,
        )

    def out_own(t, c):
        cols = pl.ds(pl.multiple_of(me * width + c * LANES, LANES), LANES)
        return pltpu.make_async_copy(
            result.at[t, c, pl.ds(pl.multiple_of(me * part, part), part), :],
            outs[t].at[:, cols], out_recv,
        )

    def out_start(t, c):
        for d in range(heads - 1):
            out_copy(t, c, d).start()
        out_own(t, c).start()

    for c in range(chunks):
        for t in range(2):
            in_wait(t, c)
            for side, other, there in sides:
                picked = pool[t, c, PATCH:2 * PATCH, :]
                for o in range(1, patches):
                    candidate = pool[t, c, (1 + o) * PATCH:(2 + o) * PATCH, :]
                    picked = jnp.where(wanted[side] == o, candidate, picked)
                halo_out[side, t, c] = picked

                @pl.when(there)
                def _():
                    halo_copy(t, c, side, other).start()

    group = LANES // HEAD_DIM

    def prepare(c):
        for t in (2, 3):
            in_wait(t, c)
            turned[t - 2, c] = rows_in[t - 2, c].T
        for h in range(group):
            head = (sub >= h * HEAD_DIM) & (sub < (h + 1) * HEAD_DIM)
            for t in range(2):
                part_t = jnp.where(head, turned[t, c], jnp.zeros((), BF16))
                block = dot(pool[t, c, PATCH:PATCH + own], part_t)
                near[t, c * group + h] = block * (SCALE * LOG2E) if t == 0 else block

    sub = lax.broadcasted_iota(jnp.int32, (LANES, own), 0)
    col = lax.broadcasted_iota(jnp.int32, (own, LANES), 1)
    for c in range(chunks):
        prepare(c)
        queries, grads = rows_in[0, c], rows_in[1, c]
        queries_t, grads_t = turned[0, c], turned[1, c]
        for side, other, there in sides:
            @pl.when(there)
            def _():
                for t in range(2):
                    halo_arrived(t, c, side, other).wait_recv()
        keys, values = pool[0, c], pool[1, c]
        keys_t, values_t = keys.T, values.T
        mixed_all, dq_all = [], []
        dk = dv = None
        for h in range(group):
            low, high = h * HEAD_DIM, (h + 1) * HEAD_DIM
            in_sub = (sub >= low) & (sub < high)
            in_col = (col >= low) & (col < high)
            zero = jnp.zeros((), BF16)
            u = c * group + h
            far_keys = jnp.concatenate([keys[:PATCH], keys[PATCH + own:]], 0)
            far_values = jnp.concatenate([values[:PATCH], values[PATCH + own:]], 0)
            far_scores = dot(far_keys, jnp.where(in_sub, queries_t, zero)) * (SCALE * LOG2E)
            far_probs = dot(far_values, jnp.where(in_sub, grads_t, zero))
            slots = [far_scores[:PATCH]]
            slots += [near[0, u, o * PATCH:(o + 1) * PATCH] for o in range(patches)]
            slots += [far_scores[PATCH:]]
            grad_probs = jnp.concatenate([far_probs[:PATCH], near[1, u], far_probs[PATCH:]], 0)
            tops = [
                jnp.where(n > 0, jnp.max(x, axis=0, keepdims=True), -jnp.inf)
                for n, x in zip(slot_counts, slots)
            ]
            top = functools.reduce(jnp.maximum, tops)
            exps = [
                jnp.exp2(x + jnp.where(n > 0, -top, -jnp.inf))
                for n, x in zip(slot_counts, slots)
            ]
            total = functools.reduce(
                jnp.add,
                [n * jnp.sum(x, axis=0, keepdims=True) for n, x in zip(slot_counts, exps)],
            )
            inverse = 1.0 / total
            probs = jnp.concatenate(
                [x * (n * inverse) for n, x in zip(slot_counts, exps)], 0
            )
            probs_low = probs.astype(BF16)
            mixed = dot(values_t[low:high], probs_low)
            row_dots = jnp.sum(
                grads_t[low:high].astype(F32) * mixed, axis=0, keepdims=True
            )
            grad_scores = (probs * (grad_probs - row_dots)).astype(BF16)
            mixed_all.append(mixed)
            dq_all.append(dot(keys_t[low:high], grad_scores) * SCALE)
            dk_h = dot(grad_scores, jnp.where(in_col, queries, zero))
            dv_h = dot(probs_low, jnp.where(in_col, grads, zero))
            dk = dk_h if dk is None else dk + dk_h
            dv = dv_h if dv is None else dv + dv_h
        for t, grad in enumerate((dk * SCALE, dv)):
            grad_out[0, t, c] = grad[:PATCH].astype(BF16)
            grad_out[1, t, c] = grad[PATCH + own:].astype(BF16)
            local_grad[t, c] = grad[PATCH:PATCH + own]
        for side, other, there in sides:
            @pl.when(there)
            def _():
                for t in range(2):
                    grad_copy(t, c, side, other).start()
        result[0, c] = jnp.concatenate(mixed_all, 0).T.astype(BF16)
        result[1, c] = jnp.concatenate(dq_all, 0).T.astype(BF16)
        out_start(0, c)
        out_start(1, c)

    for c in range(chunks):
        for side, other, there in sides:
            @pl.when(there)
            def _():
                for t in range(2):
                    grad_copy(t, c, side, other, arrived=True).wait_recv()
        for t in range(2):
            for o in range(patches):
                rows = slice(o * PATCH, (o + 1) * PATCH)
                total = local_grad[t, c, rows]
                for side in range(2):
                    total += jnp.where(wanted[side] == o, grad_in[t, c, side].astype(F32), 0.0)
                result[2 + t, c, rows] = total.astype(BF16)
            out_start(2 + t, c)

    sent = result.at[:, :, pl.ds(0, own - part), :]
    pltpu.make_async_copy(sent, sent, in_send).wait()
    for side, other, there in sides:
        @pl.when(there)
        def _():
            for out, sem in ((halo_out, halo_send), (grad_out, grad_send)):
                block = out.at[side]
                pltpu.make_async_copy(block, block, sem.at[side]).wait()
    pltpu.make_async_copy(sent, sent, out_send).wait()
    pltpu.make_async_copy(result, result, out_recv).wait()


def write_out(*refs):
    sems = refs[8]
    copies = [pltpu.make_async_copy(refs[i], refs[4 + i], sems.at[i]) for i in range(4)]
    for copy in copies:
        copy.start()
    for copy in copies:
        copy.wait()


def solution(mesh):
    heads, nodes = mesh.shape["head"], mesh.shape["node"]

    def shards(queries, key_rows, value_rows, out_grads, neighbours):
        part, model = queries.shape
        own = part * heads
        chunks = model // heads // LANES
        pool_rows = own + 2 * PATCH
        any_spec = pl.BlockSpec(memory_space=pl.ANY)
        dma = pltpu.SemaphoreType.DMA
        landed = pl.pallas_call(
            functools.partial(kernel, heads, nodes),
            out_shape=[pltpu.VMEM((part, model), BF16)] * 4,
            in_specs=[any_spec] * 5,
            out_specs=[pl.BlockSpec(memory_space=pltpu.VMEM)] * 4,
            scratch_shapes=[
                pltpu.SMEM(neighbours.shape, jnp.int32),
                dma,
                pltpu.VMEM((2, chunks, pool_rows, LANES), BF16),
                pltpu.VMEM((2, chunks, own, LANES), BF16),
                pltpu.VMEM((2, 2, chunks, PATCH, LANES), BF16),
                pltpu.VMEM((2, 2, chunks, PATCH, LANES), BF16),
                pltpu.VMEM((2, chunks, 2, PATCH, LANES), BF16),
                pltpu.VMEM((2, chunks, own, LANES), F32),
                pltpu.VMEM((4, chunks, own, LANES), BF16),
                pltpu.VMEM((2, chunks, LANES, own), BF16),
                pltpu.VMEM((2, model // heads // HEAD_DIM, own, own), F32),
                dma,
                dma((4, chunks)),
                dma((2,)),
                dma((2, chunks, 2)),
                dma((2,)),
                dma((2, chunks, 2)),
                dma,
                dma,
            ],
            compiler_params=pltpu.CompilerParams(collective_id=0, has_side_effects=True),
        )(neighbours, queries, key_rows, value_rows, out_grads)
        return pl.pallas_call(
            write_out,
            out_shape=[jax.ShapeDtypeStruct((part, model), BF16)] * 4,
            in_specs=[pl.BlockSpec(memory_space=pltpu.VMEM)] * 4,
            out_specs=[any_spec] * 4,
            scratch_shapes=[dma((4,))],
        )(*[pltpu.with_memory_space_constraint(x, pltpu.VMEM) for x in landed])

    rows = P(("grp", "node", "head"), None)
    return jax.shard_map(
        shards, mesh=mesh, in_specs=(rows, rows, rows, rows, P("grp", None)),
        out_specs=(rows,) * 4, check_vma=False,
    )
```

```python
import functools
import math

import jax
import jax.numpy as jnp
from jax import lax
from jax.experimental import pallas as pl
from jax.experimental.pallas import tpu as pltpu
from jax.sharding import PartitionSpec as P

HEAD_DIM = 64
PATCH = 128
LANES = 128
MESH = pl.DeviceIdType.MESH
SCALE = HEAD_DIM ** (-0.5)
LOG2E = math.log2(math.e)
BF16 = jnp.bfloat16
F32 = jnp.float32


def dot(a, b):
    return jnp.dot(a, b, preferred_element_type=F32)


def kernel(
    heads, nodes, nbr_hbm, q_hbm, k_hbm, v_hbm, g_hbm,
    att_hbm, dq_hbm, dk_hbm, dv_hbm,
    nbr_ref, nbr_sem, pool, rows_in, halo_out, grad_out, grad_in, result, turned, near, kept,
    in_send, in_recv, halo_send, halo_recv, grad_send, grad_recv, out_send, out_recv,
):
    me = lax.axis_index("head")
    node = lax.axis_index("node")
    has_left, has_right = node > 0, node < nodes - 1
    chunks = pool.shape[1]
    part = q_hbm.shape[0]
    own = part * heads
    patches = own // PATCH
    listed = nbr_ref.shape[1]
    width = chunks * LANES
    peers = [lax.rem(me + d, heads) for d in range(1, heads)]
    sides = ((0, node - 1, has_left), (1, node + 1, has_right))

    lists = pltpu.make_async_copy(nbr_hbm, nbr_ref, nbr_sem)
    lists.start()
    barrier = pltpu.get_barrier_semaphore()
    for peer in peers:
        pl.semaphore_signal(barrier, inc=1, device_id={"head": peer}, device_id_type=MESH)
    for _, other, there in sides:
        @pl.when(there)
        def _():
            pl.semaphore_signal(barrier, inc=1, device_id={"node": other}, device_id_type=MESH)

    sources = (k_hbm, v_hbm, q_hbm, g_hbm)

    def landing(t, c):
        if t < 2:
            return pool.at[t, c, pl.ds(pl.multiple_of(PATCH + me * part, part), part), :]
        return rows_in.at[t - 2, c, pl.ds(pl.multiple_of(me * part, part), part), :]

    def in_copy(t, c, d):
        peer = peers[d]
        cols = pl.ds(pl.multiple_of(peer * width + c * LANES, LANES), LANES)
        return pltpu.make_async_remote_copy(
            src_ref=sources[t].at[:, cols], dst_ref=landing(t, c),
            send_sem=in_send, recv_sem=in_recv.at[t, c],
            device_id={"head": peer}, device_id_type=MESH,
        )

    def in_own(t, c):
        cols = pl.ds(pl.multiple_of(me * width + c * LANES, LANES), LANES)
        return pltpu.make_async_copy(sources[t].at[:, cols], landing(t, c), in_recv.at[t, c])

    order = [(t, c) for ts in ((0, 1), (2, 3)) for c in range(chunks) for t in ts]
    for t, c in order:
        in_own(t, c).start()

    for side, _, there in sides:
        @pl.when(jnp.logical_not(there))
        def _():
            start = side * (PATCH + own)
            pool[:, :, start:start + PATCH, :] = jnp.zeros((2, chunks, PATCH, LANES), BF16)
            grad_in[:, :, side] = jnp.zeros((2, chunks, PATCH, LANES), BF16)

    pl.semaphore_wait(
        barrier, heads - 1 + has_left.astype(jnp.int32) + has_right.astype(jnp.int32)
    )
    for t, c in order:
        for d in range(heads - 1):
            in_copy(t, c, d).start()

    lists.wait()
    first = node * patches
    lane = lax.broadcasted_iota(jnp.int32, (1, own), 1)
    slot_counts = [jnp.zeros((1, own), F32) for _ in range(patches + 2)]
    for p in range(patches):
        counts = [jnp.int32(0)] * (patches + 2)
        counts[1 + p] = jnp.int32(1)
        for e in range(listed):
            value = nbr_ref[first + p, e]
            counts[0] += jnp.where(value < first, 1, 0)
            counts[-1] += jnp.where(value >= first + patches, 1, 0)
            for o in range(patches):
                counts[1 + o] += jnp.where(value == first + o, 1, 0)
        in_patch = (lane >= p * PATCH) & (lane < (p + 1) * PATCH)
        for s in range(patches + 2):
            slot_counts[s] = jnp.where(in_patch, counts[s].astype(F32), slot_counts[s])
    wanted = []
    for side, other, there in sides:
        start = jnp.clip(other, 0, nodes - 1) * patches
        pick = jnp.int32(0)
        for p in range(patches):
            for e in range(listed):
                value = nbr_ref[start + p, e]
                for o in range(1, patches):
                    pick = jnp.maximum(pick, jnp.where(value == first + o, o, 0))
        wanted.append(pick)

    def in_wait(t, c):
        if t < 2:
            whole = pool.at[t, c, pl.ds(PATCH, own), :]
        else:
            whole = rows_in.at[t - 2, c]
        pltpu.make_async_copy(whole, whole, in_recv.at[t, c]).wait()

    def halo_copy(t, c, side, other):
        start = (1 - side) * (PATCH + own)
        return pltpu.make_async_remote_copy(
            src_ref=halo_out.at[side, t, c], dst_ref=pool.at[t, c, pl.ds(start, PATCH), :],
            send_sem=halo_send.at[side], recv_sem=halo_recv.at[t, c, 1 - side],
            device_id={"node": other}, device_id_type=MESH,
        )

    def halo_arrived(t, c, side, other):
        start = side * (PATCH + own)
        return pltpu.make_async_remote_copy(
            src_ref=halo_out.at[side, t, c], dst_ref=pool.at[t, c, pl.ds(start, PATCH), :],
            send_sem=halo_send.at[side], recv_sem=halo_recv.at[t, c, side],
            device_id={"node": other}, device_id_type=MESH,
        )

    def grad_copy(t, c, side, other, arrived=False):
        far = side if arrived else 1 - side
        return pltpu.make_async_remote_copy(
            src_ref=grad_out.at[side, t, c], dst_ref=grad_in.at[t, c, far],
            send_sem=grad_send.at[side], recv_sem=grad_recv.at[t, c, far],
            device_id={"node": other}, device_id_type=MESH,
        )

    outs = (att_hbm, dq_hbm, dk_hbm, dv_hbm)

    def out_copy(t, c, d):
        peer = peers[d]
        cols = pl.ds(pl.multiple_of(me * width + c * LANES, LANES), LANES)
        return pltpu.make_async_remote_copy(
            src_ref=result.at[t, c, pl.ds(pl.multiple_of(peer * part, part), part), :],
            dst_ref=outs[t].at[:, cols],
            send_sem=out_send, recv_sem=out_recv,
            device_id={"head": peer}, device_id_type=MESH,
        )

    def out_own(t, c):
        cols = pl.ds(pl.multiple_of(me * width + c * LANES, LANES), LANES)
        return pltpu.make_async_copy(
            result.at[t, c, pl.ds(pl.multiple_of(me * part, part), part), :],
            outs[t].at[:, cols], out_recv,
        )

    def out_start(t, c):
        for d in range(heads - 1):
            out_copy(t, c, d).start()
        out_own(t, c).start()

    def forward_halo(c):
        for t in range(2):
            in_wait(t, c)
            for side, other, there in sides:
                picked = pool[t, c, PATCH:2 * PATCH, :]
                for o in range(1, patches):
                    candidate = pool[t, c, (1 + o) * PATCH:(2 + o) * PATCH, :]
                    picked = jnp.where(wanted[side] == o, candidate, picked)
                halo_out[side, t, c] = picked

                @pl.when(there)
                def _():
                    halo_copy(t, c, side, other).start()

    group = LANES // HEAD_DIM
    sub = lax.broadcasted_iota(jnp.int32, (LANES, own), 0)
    col = lax.broadcasted_iota(jnp.int32, (own, LANES), 1)
    zero = jnp.zeros((), BF16)
    span = [(h * HEAD_DIM, (h + 1) * HEAD_DIM) for h in range(group)]
    sub_heads = [(sub >= low) & (sub < high) for low, high in span]
    col_heads = [(col >= low) & (col < high) for low, high in span]
    near_counts = slot_counts[1:-1]
    far_counts = (slot_counts[0], slot_counts[-1])

    def shifted(n, x, top):
        return jnp.exp2(x + jnp.where(n > 0, -top, -jnp.inf))

    def highest(n, x):
        return jnp.where(n > 0, jnp.max(x, axis=0, keepdims=True), -jnp.inf)

    def rows_of(x, o):
        return x[o * PATCH:(o + 1) * PATCH]

    def prepare(c):
        stats = []
        for t in (2, 3):
            in_wait(t, c)
            turned[t - 2, c] = rows_in[t - 2, c].T
        for t in range(2):
            turned[2 + t, c] = pool[t, c, PATCH:PATCH + own].T
        for h in range(group):
            u = c * group + h
            scores = dot(pool[0, c, PATCH:PATCH + own], jnp.where(sub_heads[h], turned[0, c], zero))
            scores = scores * (SCALE * LOG2E)
            top = functools.reduce(
                jnp.maximum, [highest(n, rows_of(scores, o)) for o, n in enumerate(near_counts)]
            )
            total = jnp.zeros((1, own), F32)
            for o, n in enumerate(near_counts):
                x = shifted(n, rows_of(scores, o), top)
                near[0, u, o * PATCH:(o + 1) * PATCH] = x
                total += n * jnp.sum(x, axis=0, keepdims=True)
            stats.append((top, total))
            near[1, u] = dot(
                pool[1, c, PATCH:PATCH + own], jnp.where(sub_heads[h], turned[1, c], zero)
            )
        return stats

    def far_rows(t, c):
        return jnp.concatenate([pool[t, c, :PATCH], pool[t, c, PATCH + own:]], 0)

    def halo_wait(t, c):
        for side, other, there in sides:
            @pl.when(there)
            def _():
                halo_arrived(t, c, side, other).wait_recv()

    def send_grad(t, c, grad):
        for side, other, there in sides:
            grad_out[side, t, c] = rows_of(grad, side).astype(BF16)

            @pl.when(there)
            def _():
                grad_copy(t, c, side, other).start()

    def attend(c, stats):
        grads_t = turned[1, c]
        halo_wait(0, c)
        far_keys = far_rows(0, c)
        probs = []
        for h in range(group):
            u = c * group + h
            scores = dot(far_keys, jnp.where(sub_heads[h], turned[0, c], zero)) * (SCALE * LOG2E)
            near_top, near_total = stats[h]
            top = functools.reduce(
                jnp.maximum, [highest(n, rows_of(scores, i)) for i, n in enumerate(far_counts)], near_top
            )
            exps = [shifted(n, rows_of(scores, i), top) for i, n in enumerate(far_counts)]
            alpha = jnp.exp2(near_top - top)
            total = near_total * alpha
            for n, x in zip(far_counts, exps):
                total += n * jnp.sum(x, axis=0, keepdims=True)
            inverse = 1.0 / total
            far = jnp.concatenate([x * (n * inverse) for n, x in zip(far_counts, exps)], 0)
            factor = alpha * inverse
            close = jnp.concatenate(
                [near[0, u, o * PATCH:(o + 1) * PATCH] * (n * factor) for o, n in enumerate(near_counts)], 0
            )
            kept[0, u] = close.astype(BF16)
            probs.append((close, far, far.astype(BF16)))
        halo_wait(1, c)
        far_values = far_rows(1, c)
        far_values_t, far_keys_t = far_values.T, far_keys.T
        mixed = [
            dot(turned[3, c, low:high], kept[0, c * group + h]) + dot(far_values_t[low:high], probs[h][2])
            for h, (low, high) in enumerate(span)
        ]
        result[0, c] = jnp.concatenate(mixed, 0).T.astype(BF16)
        out_start(0, c)
        dv = functools.reduce(
            jnp.add,
            [dot(probs[h][2], jnp.where(col_heads[h], rows_in[1, c], zero)) for h in range(group)],
        )
        send_grad(1, c, dv)
        dq_all, dk = [], None
        for h, (low, high) in enumerate(span):
            u = c * group + h
            close, far, _ = probs[h]
            row_dots = jnp.sum(grads_t[low:high].astype(F32) * mixed[h], axis=0, keepdims=True)
            grad_far = dot(far_values, jnp.where(sub_heads[h], grads_t, zero))
            far_scores = (far * (grad_far - row_dots)).astype(BF16)
            close_scores = (close * (near[1, u] - row_dots)).astype(BF16)
            kept[1, u] = close_scores
            dk_h = dot(far_scores, jnp.where(col_heads[h], rows_in[0, c], zero))
            dk = dk_h if dk is None else dk + dk_h
            dq_all.append(
                (dot(turned[2, c, low:high], close_scores) + dot(far_keys_t[low:high], far_scores)) * SCALE
            )
        send_grad(0, c, dk * SCALE)
        result[1, c] = jnp.concatenate(dq_all, 0).T.astype(BF16)
        out_start(1, c)

    def finish(c):
        for t in (1, 0):
            total = functools.reduce(
                jnp.add,
                [
                    dot(kept[1 - t, c * group + h], jnp.where(col_heads[h], rows_in[t, c], zero))
                    for h in range(group)
                ],
            )
            if t == 0:
                total = total * SCALE
            for side, other, there in sides:
                @pl.when(there)
                def _():
                    grad_copy(t, c, side, other, arrived=True).wait_recv()
            for o in range(patches):
                rows = slice(o * PATCH, (o + 1) * PATCH)
                block = total[rows]
                for side in range(2):
                    block += jnp.where(wanted[side] == o, grad_in[t, c, side].astype(F32), 0.0)
                result[2 + t, c, rows] = block.astype(BF16)
            out_start(2 + t, c)

    for c in range(chunks):
        forward_halo(c)
    for c in range(chunks):
        attend(c, prepare(c))
    for c in range(chunks):
        finish(c)

    sent = result.at[:, :, pl.ds(0, own - part), :]
    pltpu.make_async_copy(sent, sent, in_send).wait()
    for side, other, there in sides:
        @pl.when(there)
        def _():
            for out, sem in ((halo_out, halo_send), (grad_out, grad_send)):
                block = out.at[side]
                pltpu.make_async_copy(block, block, sem.at[side]).wait()
    pltpu.make_async_copy(sent, sent, out_send).wait()
    pltpu.make_async_copy(result, result, out_recv).wait()


def write_out(*refs):
    sems = refs[8]
    copies = [pltpu.make_async_copy(refs[i], refs[4 + i], sems.at[i]) for i in range(4)]
    for copy in copies:
        copy.start()
    for copy in copies:
        copy.wait()


def solution(mesh):
    heads, nodes = mesh.shape["head"], mesh.shape["node"]

    def shards(queries, key_rows, value_rows, out_grads, neighbours):
        part, model = queries.shape
        own = part * heads
        chunks = model // heads // LANES
        pool_rows = own + 2 * PATCH
        any_spec = pl.BlockSpec(memory_space=pl.ANY)
        dma = pltpu.SemaphoreType.DMA
        landed = pl.pallas_call(
            functools.partial(kernel, heads, nodes),
            out_shape=[pltpu.VMEM((part, model), BF16)] * 4,
            in_specs=[any_spec] * 5,
            out_specs=[pl.BlockSpec(memory_space=pltpu.VMEM)] * 4,
            scratch_shapes=[
                pltpu.SMEM(neighbours.shape, jnp.int32),
                dma,
                pltpu.VMEM((2, chunks, pool_rows, LANES), BF16),
                pltpu.VMEM((2, chunks, own, LANES), BF16),
                pltpu.VMEM((2, 2, chunks, PATCH, LANES), BF16),
                pltpu.VMEM((2, 2, chunks, PATCH, LANES), BF16),
                pltpu.VMEM((2, chunks, 2, PATCH, LANES), BF16),
                pltpu.VMEM((4, chunks, own, LANES), BF16),
                pltpu.VMEM((4, chunks, LANES, own), BF16),
                pltpu.VMEM((2, model // heads // HEAD_DIM, own, own), F32),
                pltpu.VMEM((2, model // heads // HEAD_DIM, own, own), BF16),
                dma,
                dma((4, chunks)),
                dma((2,)),
                dma((2, chunks, 2)),
                dma((2,)),
                dma((2, chunks, 2)),
                dma,
                dma,
            ],
            compiler_params=pltpu.CompilerParams(collective_id=0, has_side_effects=True),
        )(neighbours, queries, key_rows, value_rows, out_grads)
        return pl.pallas_call(
            write_out,
            out_shape=[jax.ShapeDtypeStruct((part, model), BF16)] * 4,
            in_specs=[pl.BlockSpec(memory_space=pltpu.VMEM)] * 4,
            out_specs=[any_spec] * 4,
            scratch_shapes=[dma((4,))],
        )(*[pltpu.with_memory_space_constraint(x, pltpu.VMEM) for x in landed])

    rows = P(("grp", "node", "head"), None)
    return jax.shard_map(
        shards, mesh=mesh, in_specs=(rows, rows, rows, rows, P("grp", None)),
        out_specs=(rows,) * 4, check_vma=False,
    )
```

```python
import functools
import math

import jax
import jax.numpy as jnp
from jax import lax
from jax.experimental import pallas as pl
from jax.experimental.pallas import tpu as pltpu
from jax.sharding import PartitionSpec as P

HEAD_DIM = 64
PATCH = 128
LANES = 128
MESH = pl.DeviceIdType.MESH
SCALE = HEAD_DIM ** (-0.5)
LOG2E = math.log2(math.e)
BF16 = jnp.bfloat16
F32 = jnp.float32


def dot(a, b):
    return jnp.dot(a, b, preferred_element_type=F32)


def kernel(
    heads, nodes, nbr_hbm, q_hbm, k_hbm, v_hbm, g_hbm,
    att_hbm, dq_hbm, dk_hbm, dv_hbm,
    nbr_ref, nbr_sem, pool, rows_in, halo_out, grad_out, grad_in, result, turned, near, kept,
    ready, in_send, in_recv, halo_send, halo_recv, grad_send, grad_recv, out_send, out_recv,
):
    me = lax.axis_index("head")
    node = lax.axis_index("node")
    has_left, has_right = node > 0, node < nodes - 1
    chunks = pool.shape[1]
    part = q_hbm.shape[0]
    own = part * heads
    patches = own // PATCH
    listed = nbr_ref.shape[1]
    width = chunks * LANES
    peers = [lax.rem(me + d, heads) for d in range(1, heads)]
    sides = ((0, node - 1, has_left), (1, node + 1, has_right))

    lists = pltpu.make_async_copy(nbr_hbm, nbr_ref, nbr_sem)
    lists.start()
    barrier = pltpu.get_barrier_semaphore()
    for peer in peers:
        pl.semaphore_signal(barrier, inc=1, device_id={"head": peer}, device_id_type=MESH)

    @pl.when(has_right)
    def _():
        pl.semaphore_signal(barrier, inc=1, device_id={"node": node + 1}, device_id_type=MESH)

    sources = (k_hbm, v_hbm, q_hbm, g_hbm)

    def landing(t, c):
        if t < 2:
            return pool.at[t, c, pl.ds(pl.multiple_of(PATCH + me * part, part), part), :]
        return rows_in.at[t - 2, c, pl.ds(pl.multiple_of(me * part, part), part), :]

    def in_copy(t, c, d):
        peer = peers[d]
        cols = pl.ds(pl.multiple_of(peer * width + c * LANES, LANES), LANES)
        return pltpu.make_async_remote_copy(
            src_ref=sources[t].at[:, cols], dst_ref=landing(t, c),
            send_sem=in_send, recv_sem=in_recv.at[t, c],
            device_id={"head": peer}, device_id_type=MESH,
        )

    def in_own(t, c):
        cols = pl.ds(pl.multiple_of(me * width + c * LANES, LANES), LANES)
        return pltpu.make_async_copy(sources[t].at[:, cols], landing(t, c), in_recv.at[t, c])

    order = [(t, c) for ts in ((0, 1), (2, 3)) for c in range(chunks) for t in ts]

    for side, _, there in sides:
        @pl.when(jnp.logical_not(there))
        def _():
            start = side * (PATCH + own)
            pool[:, :, start:start + PATCH, :] = jnp.zeros((2, chunks, PATCH, LANES), BF16)
            grad_in[:, :, side] = jnp.zeros((2, chunks, PATCH, LANES), BF16)

    pl.semaphore_wait(barrier, heads - 1 + has_left.astype(jnp.int32))

    @pl.when(has_left)
    def _():
        pl.semaphore_signal(ready, inc=1, device_id={"node": node - 1}, device_id_type=MESH)

    for t, c in order:
        for d in range(heads - 1):
            in_copy(t, c, d).start()
    for t, c in order:
        in_own(t, c).start()

    lists.wait()
    first = node * patches
    lane = lax.broadcasted_iota(jnp.int32, (1, own), 1)
    slot_counts = [jnp.zeros((1, own), F32) for _ in range(patches + 2)]
    for p in range(patches):
        counts = [jnp.int32(0)] * (patches + 2)
        counts[1 + p] = jnp.int32(1)
        for e in range(listed):
            value = nbr_ref[first + p, e]
            counts[0] += jnp.where(value < first, 1, 0)
            counts[-1] += jnp.where(value >= first + patches, 1, 0)
            for o in range(patches):
                counts[1 + o] += jnp.where(value == first + o, 1, 0)
        in_patch = (lane >= p * PATCH) & (lane < (p + 1) * PATCH)
        for s in range(patches + 2):
            slot_counts[s] = jnp.where(in_patch, counts[s].astype(F32), slot_counts[s])
    wanted = []
    for side, other, there in sides:
        start = jnp.clip(other, 0, nodes - 1) * patches
        pick = jnp.int32(0)
        for p in range(patches):
            for e in range(listed):
                value = nbr_ref[start + p, e]
                for o in range(1, patches):
                    pick = jnp.maximum(pick, jnp.where(value == first + o, o, 0))
        wanted.append(pick)

    def in_wait(t, c):
        if t < 2:
            whole = pool.at[t, c, pl.ds(PATCH, own), :]
        else:
            whole = rows_in.at[t - 2, c]
        pltpu.make_async_copy(whole, whole, in_recv.at[t, c]).wait()

    def halo_copy(t, c, side, other):
        start = (1 - side) * (PATCH + own)
        return pltpu.make_async_remote_copy(
            src_ref=halo_out.at[side, t, c], dst_ref=pool.at[t, c, pl.ds(start, PATCH), :],
            send_sem=halo_send.at[side], recv_sem=halo_recv.at[t, c, 1 - side],
            device_id={"node": other}, device_id_type=MESH,
        )

    def halo_arrived(t, c, side, other):
        start = side * (PATCH + own)
        return pltpu.make_async_remote_copy(
            src_ref=halo_out.at[side, t, c], dst_ref=pool.at[t, c, pl.ds(start, PATCH), :],
            send_sem=halo_send.at[side], recv_sem=halo_recv.at[t, c, side],
            device_id={"node": other}, device_id_type=MESH,
        )

    def grad_copy(t, c, side, other, arrived=False):
        far = side if arrived else 1 - side
        return pltpu.make_async_remote_copy(
            src_ref=grad_out.at[side, t, c], dst_ref=grad_in.at[t, c, far],
            send_sem=grad_send.at[side], recv_sem=grad_recv.at[t, c, far],
            device_id={"node": other}, device_id_type=MESH,
        )

    outs = (att_hbm, dq_hbm, dk_hbm, dv_hbm)

    def out_copy(t, c, d):
        peer = peers[d]
        cols = pl.ds(pl.multiple_of(me * width + c * LANES, LANES), LANES)
        return pltpu.make_async_remote_copy(
            src_ref=result.at[t, c, pl.ds(pl.multiple_of(peer * part, part), part), :],
            dst_ref=outs[t].at[:, cols],
            send_sem=out_send, recv_sem=out_recv,
            device_id={"head": peer}, device_id_type=MESH,
        )

    def out_own(t, c):
        cols = pl.ds(pl.multiple_of(me * width + c * LANES, LANES), LANES)
        return pltpu.make_async_copy(
            result.at[t, c, pl.ds(pl.multiple_of(me * part, part), part), :],
            outs[t].at[:, cols], out_recv,
        )

    def out_start(t, c):
        for d in range(heads - 1):
            out_copy(t, c, d).start()
        out_own(t, c).start()

    def forward_halo(c):
        for t in range(2):
            in_wait(t, c)
            for side, other, there in sides:
                picked = pool[t, c, PATCH:2 * PATCH, :]
                for o in range(1, patches):
                    candidate = pool[t, c, (1 + o) * PATCH:(2 + o) * PATCH, :]
                    picked = jnp.where(wanted[side] == o, candidate, picked)
                halo_out[side, t, c] = picked

                @pl.when(there)
                def _():
                    halo_copy(t, c, side, other).start()

    group = LANES // HEAD_DIM
    sub = lax.broadcasted_iota(jnp.int32, (LANES, own), 0)
    col = lax.broadcasted_iota(jnp.int32, (own, LANES), 1)
    zero = jnp.zeros((), BF16)
    span = [(h * HEAD_DIM, (h + 1) * HEAD_DIM) for h in range(group)]
    sub_heads = [(sub >= low) & (sub < high) for low, high in span]
    col_heads = [(col >= low) & (col < high) for low, high in span]
    near_counts = slot_counts[1:-1]
    far_counts = (slot_counts[0], slot_counts[-1])

    def shifted(n, x, top):
        return jnp.exp2(x + jnp.where(n > 0, -top, -jnp.inf))

    def highest(n, x):
        return jnp.where(n > 0, jnp.max(x, axis=0, keepdims=True), -jnp.inf)

    def rows_of(x, o):
        return x[o * PATCH:(o + 1) * PATCH]

    def prepare(c):
        stats = []
        in_wait(2, c)
        turned[0, c] = rows_in[0, c].T
        for h in range(group):
            u = c * group + h
            scores = dot(pool[0, c, PATCH:PATCH + own], jnp.where(sub_heads[h], turned[0, c], zero))
            scores = scores * (SCALE * LOG2E)
            top = functools.reduce(
                jnp.maximum, [highest(n, rows_of(scores, o)) for o, n in enumerate(near_counts)]
            )
            total = jnp.zeros((1, own), F32)
            for o, n in enumerate(near_counts):
                x = shifted(n, rows_of(scores, o), top)
                near[u, o * PATCH:(o + 1) * PATCH] = x
                total += n * jnp.sum(x, axis=0, keepdims=True)
            stats.append((top, total))
        return stats

    def far_rows(t, c):
        return jnp.concatenate([pool[t, c, :PATCH], pool[t, c, PATCH + own:]], 0)

    def halo_wait(t, c):
        for side, other, there in sides:
            @pl.when(there)
            def _():
                halo_arrived(t, c, side, other).wait_recv()

    def send_grad(t, c, grad):
        for side, other, there in sides:
            grad_out[side, t, c] = rows_of(grad, side).astype(BF16)

            @pl.when(there)
            def _():
                grad_copy(t, c, side, other).start()

    def attend(c, stats):
        halo_wait(0, c)
        far_keys = far_rows(0, c)
        probs = []
        for h in range(group):
            u = c * group + h
            scores = dot(far_keys, jnp.where(sub_heads[h], turned[0, c], zero)) * (SCALE * LOG2E)
            near_top, near_total = stats[h]
            top = functools.reduce(
                jnp.maximum, [highest(n, rows_of(scores, i)) for i, n in enumerate(far_counts)], near_top
            )
            exps = [shifted(n, rows_of(scores, i), top) for i, n in enumerate(far_counts)]
            alpha = jnp.exp2(near_top - top)
            total = near_total * alpha
            for n, x in zip(far_counts, exps):
                total += n * jnp.sum(x, axis=0, keepdims=True)
            inverse = 1.0 / total
            far = jnp.concatenate([x * (n * inverse) for n, x in zip(far_counts, exps)], 0)
            factor = alpha * inverse
            close = jnp.concatenate(
                [near[u, o * PATCH:(o + 1) * PATCH] * (n * factor) for o, n in enumerate(near_counts)], 0
            )
            kept[0, u] = close.astype(BF16)
            probs.append((close, far, far.astype(BF16)))
        halo_wait(1, c)
        far_values = far_rows(1, c)
        far_values_t = far_values.T
        mixed = [
            dot(turned[3, c, low:high], kept[0, c * group + h]) + dot(far_values_t[low:high], probs[h][2])
            for h, (low, high) in enumerate(span)
        ]
        result[0, c] = jnp.concatenate(mixed, 0).T.astype(BF16)
        out_start(0, c)
        in_wait(3, c)
        turned[1, c] = rows_in[1, c].T
        grads_t = turned[1, c]
        dv = functools.reduce(
            jnp.add,
            [dot(probs[h][2], jnp.where(col_heads[h], rows_in[1, c], zero)) for h in range(group)],
        )
        send_grad(1, c, dv)
        far_keys_t = far_keys.T
        dq_all, dk = [], None
        for h, (low, high) in enumerate(span):
            u = c * group + h
            close, far, _ = probs[h]
            row_dots = jnp.sum(grads_t[low:high].astype(F32) * mixed[h], axis=0, keepdims=True)
            grad_far = dot(far_values, jnp.where(sub_heads[h], grads_t, zero))
            far_scores = (far * (grad_far - row_dots)).astype(BF16)
            grad_near = dot(pool[1, c, PATCH:PATCH + own], jnp.where(sub_heads[h], grads_t, zero))
            close_scores = (close * (grad_near - row_dots)).astype(BF16)
            kept[1, u] = close_scores
            dk_h = dot(far_scores, jnp.where(col_heads[h], rows_in[0, c], zero))
            dk = dk_h if dk is None else dk + dk_h
            dq_all.append(
                (dot(turned[2, c, low:high], close_scores) + dot(far_keys_t[low:high], far_scores)) * SCALE
            )
        send_grad(0, c, dk * SCALE)
        result[1, c] = jnp.concatenate(dq_all, 0).T.astype(BF16)
        out_start(1, c)

    def finish(c):
        for t in (1, 0):
            total = functools.reduce(
                jnp.add,
                [
                    dot(kept[1 - t, c * group + h], jnp.where(col_heads[h], rows_in[t, c], zero))
                    for h in range(group)
                ],
            )
            if t == 0:
                total = total * SCALE
            for side, other, there in sides:
                @pl.when(there)
                def _():
                    grad_copy(t, c, side, other, arrived=True).wait_recv()
            for o in range(patches):
                rows = slice(o * PATCH, (o + 1) * PATCH)
                block = total[rows]
                for side in range(2):
                    block += jnp.where(wanted[side] == o, grad_in[t, c, side].astype(F32), 0.0)
                result[2 + t, c, rows] = block.astype(BF16)
            out_start(2 + t, c)

    @pl.when(has_right)
    def _():
        pl.semaphore_wait(ready, 1)

    for c in range(chunks):
        forward_halo(c)
    for c in range(chunks):
        for t in range(2):
            turned[2 + t, c] = pool[t, c, PATCH:PATCH + own].T
    for c in range(chunks):
        attend(c, prepare(c))
    for c in range(chunks):
        finish(c)

    sent = result.at[:, :, pl.ds(0, own - part), :]
    pltpu.make_async_copy(sent, sent, in_send).wait()
    for side, other, there in sides:
        @pl.when(there)
        def _():
            for out, sem in ((halo_out, halo_send), (grad_out, grad_send)):
                block = out.at[side]
                pltpu.make_async_copy(block, block, sem.at[side]).wait()
    pltpu.make_async_copy(sent, sent, out_send).wait()
    pltpu.make_async_copy(result, result, out_recv).wait()


def write_out(*refs):
    sems = refs[8]
    copies = [pltpu.make_async_copy(refs[i], refs[4 + i], sems.at[i]) for i in range(4)]
    for copy in copies:
        copy.start()
    for copy in copies:
        copy.wait()


def solution(mesh):
    heads, nodes = mesh.shape["head"], mesh.shape["node"]

    def shards(queries, key_rows, value_rows, out_grads, neighbours):
        part, model = queries.shape
        own = part * heads
        chunks = model // heads // LANES
        pool_rows = own + 2 * PATCH
        any_spec = pl.BlockSpec(memory_space=pl.ANY)
        dma = pltpu.SemaphoreType.DMA
        landed = pl.pallas_call(
            functools.partial(kernel, heads, nodes),
            out_shape=[pltpu.VMEM((part, model), BF16)] * 4,
            in_specs=[any_spec] * 5,
            out_specs=[pl.BlockSpec(memory_space=pltpu.VMEM)] * 4,
            scratch_shapes=[
                pltpu.SMEM(neighbours.shape, jnp.int32),
                dma,
                pltpu.VMEM((2, chunks, pool_rows, LANES), BF16),
                pltpu.VMEM((2, chunks, own, LANES), BF16),
                pltpu.VMEM((2, 2, chunks, PATCH, LANES), BF16),
                pltpu.VMEM((2, 2, chunks, PATCH, LANES), BF16),
                pltpu.VMEM((2, chunks, 2, PATCH, LANES), BF16),
                pltpu.VMEM((4, chunks, own, LANES), BF16),
                pltpu.VMEM((4, chunks, LANES, own), BF16),
                pltpu.VMEM((model // heads // HEAD_DIM, own, own), F32),
                pltpu.VMEM((2, model // heads // HEAD_DIM, own, own), BF16),
                pltpu.SemaphoreType.REGULAR,
                dma,
                dma((4, chunks)),
                dma((2,)),
                dma((2, chunks, 2)),
                dma((2,)),
                dma((2, chunks, 2)),
                dma,
                dma,
            ],
            compiler_params=pltpu.CompilerParams(collective_id=0, has_side_effects=True),
        )(neighbours, queries, key_rows, value_rows, out_grads)
        return pl.pallas_call(
            write_out,
            out_shape=[jax.ShapeDtypeStruct((part, model), BF16)] * 4,
            in_specs=[pl.BlockSpec(memory_space=pltpu.VMEM)] * 4,
            out_specs=[any_spec] * 4,
            scratch_shapes=[dma((4,))],
        )(*[pltpu.with_memory_space_constraint(x, pltpu.VMEM) for x in landed])

    rows = P(("grp", "node", "head"), None)
    return jax.shard_map(
        shards, mesh=mesh, in_specs=(rows, rows, rows, rows, P("grp", None)),
        out_specs=(rows,) * 4, check_vma=False,
    )
```

```python
import functools
import math

import jax
import jax.numpy as jnp
from jax import lax
from jax.experimental import pallas as pl
from jax.experimental.pallas import tpu as pltpu
from jax.sharding import PartitionSpec as P

HEAD_DIM = 64
PATCH = 128
LANES = 128
MESH = pl.DeviceIdType.MESH
SCALE = HEAD_DIM ** (-0.5)
LOG2E = math.log2(math.e)
BF16 = jnp.bfloat16
F32 = jnp.float32


def dot(a, b):
    return jnp.dot(a, b, preferred_element_type=F32)


def kernel(
    heads, nodes, nbr_hbm, q_hbm, k_hbm, v_hbm, g_hbm,
    landed,
    nbr_ref, nbr_sem, pool, rows_in, halo_out, grad_out, grad_in, result, turned, near, kept,
    ready, in_send, in_recv, halo_send, halo_recv, grad_send, grad_recv, out_send, out_recv,
):
    me = lax.axis_index("head")
    node = lax.axis_index("node")
    has_left, has_right = node > 0, node < nodes - 1
    chunks = pool.shape[1]
    part = q_hbm.shape[0]
    own = part * heads
    patches = own // PATCH
    listed = nbr_ref.shape[1]
    width = chunks * LANES
    peers = [lax.rem(me + d, heads) for d in range(1, heads)]
    sides = ((0, node - 1, has_left), (1, node + 1, has_right))

    lists = pltpu.make_async_copy(nbr_hbm, nbr_ref, nbr_sem)
    lists.start()
    barrier = pltpu.get_barrier_semaphore()
    for peer in peers:
        pl.semaphore_signal(barrier, inc=1, device_id={"head": peer}, device_id_type=MESH)

    @pl.when(has_right)
    def _():
        pl.semaphore_signal(barrier, inc=1, device_id={"node": node + 1}, device_id_type=MESH)

    sources = (k_hbm, v_hbm, q_hbm, g_hbm)

    def landing(t, c):
        if t < 2:
            return pool.at[t, c, pl.ds(pl.multiple_of(PATCH + me * part, part), part), :]
        return rows_in.at[t - 2, c, pl.ds(pl.multiple_of(me * part, part), part), :]

    def in_copy(t, c, d):
        peer = peers[d]
        cols = pl.ds(pl.multiple_of(peer * width + c * LANES, LANES), LANES)
        return pltpu.make_async_remote_copy(
            src_ref=sources[t].at[:, cols], dst_ref=landing(t, c),
            send_sem=in_send, recv_sem=in_recv.at[t, c],
            device_id={"head": peer}, device_id_type=MESH,
        )

    def in_own(t, c):
        cols = pl.ds(pl.multiple_of(me * width + c * LANES, LANES), LANES)
        return pltpu.make_async_copy(sources[t].at[:, cols], landing(t, c), in_recv.at[t, c])

    order = [(t, c) for ts in ((0, 1), (2, 3)) for c in range(chunks) for t in ts]

    pl.semaphore_wait(barrier, heads - 1 + has_left.astype(jnp.int32))

    @pl.when(has_left)
    def _():
        pl.semaphore_signal(ready, inc=1, device_id={"node": node - 1}, device_id_type=MESH)

    for t, c in order:
        for d in range(heads - 1):
            in_copy(t, c, d).start()
    for t, c in order:
        in_own(t, c).start()

    for side, _, there in sides:
        @pl.when(jnp.logical_not(there))
        def _():
            start = side * (PATCH + own)
            pool[:, :, start:start + PATCH, :] = jnp.zeros((2, chunks, PATCH, LANES), BF16)
            grad_in[:, :, side] = jnp.zeros((2, chunks, PATCH, LANES), BF16)

    lists.wait()
    first = node * patches
    lane = lax.broadcasted_iota(jnp.int32, (1, own), 1)
    slot_counts = [jnp.zeros((1, own), F32) for _ in range(patches + 2)]
    for p in range(patches):
        counts = [jnp.int32(0)] * (patches + 2)
        counts[1 + p] = jnp.int32(1)
        for e in range(listed):
            value = nbr_ref[first + p, e]
            counts[0] += jnp.where(value < first, 1, 0)
            counts[-1] += jnp.where(value >= first + patches, 1, 0)
            for o in range(patches):
                counts[1 + o] += jnp.where(value == first + o, 1, 0)
        in_patch = (lane >= p * PATCH) & (lane < (p + 1) * PATCH)
        for s in range(patches + 2):
            slot_counts[s] = jnp.where(in_patch, counts[s].astype(F32), slot_counts[s])
    wanted = []
    for side, other, there in sides:
        start = jnp.clip(other, 0, nodes - 1) * patches
        pick = jnp.int32(0)
        for p in range(patches):
            for e in range(listed):
                value = nbr_ref[start + p, e]
                for o in range(1, patches):
                    pick = jnp.maximum(pick, jnp.where(value == first + o, o, 0))
        wanted.append(pick)

    def in_wait(t, c):
        if t < 2:
            whole = pool.at[t, c, pl.ds(PATCH, own), :]
        else:
            whole = rows_in.at[t - 2, c]
        pltpu.make_async_copy(whole, whole, in_recv.at[t, c]).wait()

    def halo_copy(t, c, side, other):
        start = (1 - side) * (PATCH + own)
        return pltpu.make_async_remote_copy(
            src_ref=halo_out.at[side, t, c], dst_ref=pool.at[t, c, pl.ds(start, PATCH), :],
            send_sem=halo_send, recv_sem=halo_recv.at[t, c],
            device_id={"node": other}, device_id_type=MESH,
        )

    def sides_wait(two, one, sem):
        @pl.when(has_left & has_right)
        def _():
            pltpu.make_async_copy(two, two, sem).wait()

        @pl.when(has_left != has_right)
        def _():
            pltpu.make_async_copy(one, one, sem).wait()

    def grad_copy(t, c, side, other):
        return pltpu.make_async_remote_copy(
            src_ref=grad_out.at[side, t, c], dst_ref=grad_in.at[t, c, 1 - side],
            send_sem=grad_send, recv_sem=grad_recv.at[t, c],
            device_id={"node": other}, device_id_type=MESH,
        )

    outs = [landed.at[t] for t in range(4)]

    def out_copy(t, c, d):
        peer = peers[d]
        cols = pl.ds(pl.multiple_of(me * width + c * LANES, LANES), LANES)
        return pltpu.make_async_remote_copy(
            src_ref=result.at[t, c, pl.ds(pl.multiple_of(peer * part, part), part), :],
            dst_ref=outs[t].at[:, cols],
            send_sem=out_send, recv_sem=out_recv,
            device_id={"head": peer}, device_id_type=MESH,
        )

    def out_own(t, c):
        cols = pl.ds(pl.multiple_of(me * width + c * LANES, LANES), LANES)
        return pltpu.make_async_copy(
            result.at[t, c, pl.ds(pl.multiple_of(me * part, part), part), :],
            outs[t].at[:, cols], out_recv,
        )

    def out_start(t, c):
        for d in range(heads - 1):
            out_copy(t, c, d).start()
        out_own(t, c).start()

    def forward_halo(c):
        for t in range(2):
            in_wait(t, c)
            for side, other, there in sides:
                picked = pool[t, c, PATCH:2 * PATCH, :]
                for o in range(1, patches):
                    candidate = pool[t, c, (1 + o) * PATCH:(2 + o) * PATCH, :]
                    picked = jnp.where(wanted[side] == o, candidate, picked)
                halo_out[side, t, c] = picked

                @pl.when(there)
                def _():
                    halo_copy(t, c, side, other).start()

    group = LANES // HEAD_DIM
    sub = lax.broadcasted_iota(jnp.int32, (LANES, own), 0)
    col = lax.broadcasted_iota(jnp.int32, (own, LANES), 1)
    zero = jnp.zeros((), BF16)
    span = [(h * HEAD_DIM, (h + 1) * HEAD_DIM) for h in range(group)]
    sub_heads = [(sub >= low) & (sub < high) for low, high in span]
    col_heads = [(col >= low) & (col < high) for low, high in span]
    near_counts = slot_counts[1:-1]
    far_counts = (slot_counts[0], slot_counts[-1])

    def shifted(n, x, top):
        return jnp.exp2(x + jnp.where(n > 0, -top, -jnp.inf))

    def highest(n, x):
        return jnp.where(n > 0, jnp.max(x, axis=0, keepdims=True), -jnp.inf)

    def rows_of(x, o):
        return x[o * PATCH:(o + 1) * PATCH]

    def prepare(c):
        stats = []
        in_wait(2, c)
        turned[0, c] = rows_in[0, c].T
        for h in range(group):
            u = c * group + h
            scores = dot(pool[0, c, PATCH:PATCH + own], jnp.where(sub_heads[h], turned[0, c], zero))
            scores = scores * (SCALE * LOG2E)
            top = functools.reduce(
                jnp.maximum, [highest(n, rows_of(scores, o)) for o, n in enumerate(near_counts)]
            )
            total = jnp.zeros((1, own), F32)
            for o, n in enumerate(near_counts):
                x = shifted(n, rows_of(scores, o), top)
                near[u, o * PATCH:(o + 1) * PATCH] = x
                total += n * jnp.sum(x, axis=0, keepdims=True)
            stats.append((top, total))
        return stats

    def far_rows(t, c):
        return jnp.concatenate([pool[t, c, :PATCH], pool[t, c, PATCH + own:]], 0)

    def halo_wait(t, c):
        block = pool.at[t, c]
        sides_wait(block.at[pl.ds(0, 2 * PATCH)], block.at[pl.ds(0, PATCH)], halo_recv.at[t, c])

    def send_grad(t, c, grad):
        for side, other, there in sides:
            grad_out[side, t, c] = rows_of(grad, side).astype(BF16)

            @pl.when(there)
            def _():
                grad_copy(t, c, side, other).start()

    def attend(c, stats):
        halo_wait(0, c)
        far_keys = far_rows(0, c)
        probs = []
        for h in range(group):
            u = c * group + h
            scores = dot(far_keys, jnp.where(sub_heads[h], turned[0, c], zero)) * (SCALE * LOG2E)
            near_top, near_total = stats[h]
            top = functools.reduce(
                jnp.maximum, [highest(n, rows_of(scores, i)) for i, n in enumerate(far_counts)], near_top
            )
            exps = [shifted(n, rows_of(scores, i), top) for i, n in enumerate(far_counts)]
            alpha = jnp.exp2(near_top - top)
            total = near_total * alpha
            for n, x in zip(far_counts, exps):
                total += n * jnp.sum(x, axis=0, keepdims=True)
            inverse = 1.0 / total
            far = jnp.concatenate([x * (n * inverse) for n, x in zip(far_counts, exps)], 0)
            factor = alpha * inverse
            close = jnp.concatenate(
                [near[u, o * PATCH:(o + 1) * PATCH] * (n * factor) for o, n in enumerate(near_counts)], 0
            )
            kept[0, u] = close.astype(BF16)
            probs.append((close, far, far.astype(BF16)))
        halo_wait(1, c)
        far_values = far_rows(1, c)
        far_values_t = far_values.T
        mixed = [
            dot(turned[3, c, low:high], kept[0, c * group + h]) + dot(far_values_t[low:high], probs[h][2])
            for h, (low, high) in enumerate(span)
        ]
        result[0, c] = jnp.concatenate(mixed, 0).astype(BF16).T
        out_start(0, c)
        in_wait(3, c)
        turned[1, c] = rows_in[1, c].T
        grads_t = turned[1, c]
        dv = functools.reduce(
            jnp.add,
            [dot(probs[h][2], jnp.where(col_heads[h], rows_in[1, c], zero)) for h in range(group)],
        )
        send_grad(1, c, dv)
        far_keys_t = far_keys.T
        dq_all, dk = [], None
        for h, (low, high) in enumerate(span):
            u = c * group + h
            close, far, _ = probs[h]
            row_dots = jnp.sum(grads_t[low:high].astype(F32) * mixed[h], axis=0, keepdims=True)
            grad_far = dot(far_values, jnp.where(sub_heads[h], grads_t, zero))
            far_scores = (far * (grad_far - row_dots)).astype(BF16)
            grad_near = dot(pool[1, c, PATCH:PATCH + own], jnp.where(sub_heads[h], grads_t, zero))
            close_scores = (close * (grad_near - row_dots)).astype(BF16)
            kept[1, u] = close_scores
            dk_h = dot(far_scores, jnp.where(col_heads[h], rows_in[0, c], zero))
            dk = dk_h if dk is None else dk + dk_h
            dq_all.append(
                (dot(turned[2, c, low:high], close_scores) + dot(far_keys_t[low:high], far_scores)) * SCALE
            )
        send_grad(0, c, dk * SCALE)
        result[1, c] = jnp.concatenate(dq_all, 0).astype(BF16).T
        out_start(1, c)

    def finish(c):
        for t in (1, 0):
            total = functools.reduce(
                jnp.add,
                [
                    dot(kept[1 - t, c * group + h], jnp.where(col_heads[h], rows_in[t, c], zero))
                    for h in range(group)
                ],
            )
            if t == 0:
                total = total * SCALE
            sides_wait(grad_in.at[t, c], grad_in.at[t, c, 0], grad_recv.at[t, c])
            for o in range(patches):
                rows = slice(o * PATCH, (o + 1) * PATCH)
                block = total[rows]
                for side in range(2):
                    block += jnp.where(wanted[side] == o, grad_in[t, c, side].astype(F32), 0.0)
                result[2 + t, c, rows] = block.astype(BF16)
            out_start(2 + t, c)

    @pl.when(has_right)
    def _():
        pl.semaphore_wait(ready, 1)

    for c in range(chunks):
        forward_halo(c)
    for c in range(chunks):
        for t in range(2):
            turned[2 + t, c] = pool[t, c, PATCH:PATCH + own].T
    for c in range(chunks):
        attend(c, prepare(c))
    for c in range(chunks):
        finish(c)

    sent = result.at[:, :, pl.ds(0, own - part), :]
    pltpu.make_async_copy(sent, sent, in_send).wait()
    sides_wait(halo_out, halo_out.at[0], halo_send)
    sides_wait(grad_out, grad_out.at[0], grad_send)
    pltpu.make_async_copy(sent, sent, out_send).wait()
    pltpu.make_async_copy(result, result, out_recv).wait()


def write_out(landed, *refs):
    *outs, sem = refs
    for t, out in enumerate(outs):
        pltpu.make_async_copy(landed.at[t], out, sem).start()
    pltpu.make_async_copy(landed, landed, sem).wait()


def solution(mesh):
    heads, nodes = mesh.shape["head"], mesh.shape["node"]

    def shards(queries, key_rows, value_rows, out_grads, neighbours):
        part, model = queries.shape
        own = part * heads
        chunks = model // heads // LANES
        pool_rows = own + 2 * PATCH
        any_spec = pl.BlockSpec(memory_space=pl.ANY)
        dma = pltpu.SemaphoreType.DMA
        landed = pl.pallas_call(
            functools.partial(kernel, heads, nodes),
            out_shape=pltpu.VMEM((4, part, model), BF16),
            in_specs=[any_spec] * 5,
            out_specs=pl.BlockSpec(memory_space=pltpu.VMEM),
            scratch_shapes=[
                pltpu.SMEM(neighbours.shape, jnp.int32),
                dma,
                pltpu.VMEM((2, chunks, pool_rows, LANES), BF16),
                pltpu.VMEM((2, chunks, own, LANES), BF16),
                pltpu.VMEM((2, 2, chunks, PATCH, LANES), BF16),
                pltpu.VMEM((2, 2, chunks, PATCH, LANES), BF16),
                pltpu.VMEM((2, chunks, 2, PATCH, LANES), BF16),
                pltpu.VMEM((4, chunks, own, LANES), BF16),
                pltpu.VMEM((4, chunks, LANES, own), BF16),
                pltpu.VMEM((model // heads // HEAD_DIM, own, own), F32),
                pltpu.VMEM((2, model // heads // HEAD_DIM, own, own), BF16),
                pltpu.SemaphoreType.REGULAR,
                dma,
                dma((4, chunks)),
                dma,
                dma((2, chunks)),
                dma,
                dma((2, chunks)),
                dma,
                dma,
            ],
            compiler_params=pltpu.CompilerParams(collective_id=0, has_side_effects=True),
        )(neighbours, queries, key_rows, value_rows, out_grads)
        return pl.pallas_call(
            write_out,
            out_shape=[jax.ShapeDtypeStruct((part, model), BF16)] * 4,
            in_specs=[pl.BlockSpec(memory_space=pltpu.VMEM)],
            out_specs=[any_spec] * 4,
            scratch_shapes=[dma],
        )(pltpu.with_memory_space_constraint(landed, pltpu.VMEM))

    rows = P(("grp", "node", "head"), None)
    return jax.shard_map(
        shards, mesh=mesh, in_specs=(rows, rows, rows, rows, P("grp", None)),
        out_specs=(rows,) * 4, check_vma=False,
    )
```
